256 devices in a mesh: ctx: 32 (over z_hi, y, x), tp: 8 (over z_lo, core).
Axes of the slice: x: 4, y: 4, z: 8 (z_hi: 2, z_lo: 4; z = z_hi * 4 + z_lo), core: 2. Of those that a mesh axis runs over, the one named last changes fastest.
Arguments:
- query_rows: bfloat16 [8192, 8192], P(('ctx', 'tp')), may hold values from -2 to 2
- key_rows: bfloat16 [8192, 1024], P(('ctx', 'tp')), may hold values from -2 to 2
- value_rows: bfloat16 [8192, 1024], P(('ctx', 'tp')), may hold values from -6 to 6
- doc_ids: int32 [64], replicated, may hold values from 0 to 15, never falling along the last dimension, each value on 1 to 14 neighbouring positions
- grad_out: bfloat16 [8192, 8192], P(('ctx', 'tp')), may hold values from -6 to 6
Outputs:
- attention: bfloat16 [8192, 8192], P(('ctx', 'tp'))
- grad_queries: float32 [8192, 8192], P(('ctx', 'tp'))
- grad_keys: float32 [8192, 1024], P(('ctx', 'tp'))
- grad_values: float32 [8192, 1024], P(('ctx', 'tp'))
The draws below stay inside these ranges and needn't reach their ends.
Inputs may be any that keep to these rules, and one draw needn't show every extreme that they name: `doc_ids`: block document ids never fall; each document covers 1 to 14 whole blocks, and some document exactly 14.
All inputs are finite; a program needn't handle non-finite values.
Results may differ from the reference program's by a relative error of at most 0.0048.
Values may be sent and summed in bfloat16 or wider, within the bound.
A program may use at most 128 MiB of HBM per device.

```python
import math
import jax
import jax.numpy as jnp
import numpy as np
from jax import lax

HEADS = 64
KV_HEADS = 8
HEAD_DIM = 128
BLOCK = 128
WINDOW = 8
TOK_DEV = 256
TOKENS = 8192
NBLK = 64
DOC_BLOCKS = 14
DOCS = 16
N_CTX = 32


def block_levels(own_key, extent, shards, low, high):
    loudness = 1.0
    for position, blocks in shards:
        heights = jax.random.uniform(jax.random.fold_in(jax.random.fold_in(own_key, 6), position), (blocks,), jnp.float32, low / len(shards), high / len(shards))
        loudness = loudness * jnp.repeat(jnp.exp(heights), extent[position] // blocks).reshape((-1,) + (1,) * (len(extent) - 1 - position))
    return loudness


def length_profile(number_of, total, most, skew):
    weights = [(1 << 20) // math.isqrt(rank ** skew) + 1 for rank in range(2, number_of + 1)]
    spare, holding = total - most - (number_of - 1), [1] * (number_of - 1)
    while spare > 0:
        candidates = [i for i in range(number_of - 1) if holding[i] < most]
        mass, remaining = sum([weights[i] for i in candidates]), spare
        for i in candidates:
            more = min(most - holding[i], max(1, remaining * weights[i] // mass), spare)
            holding[i] = holding[i] + more
            spare = spare - more
    return np.array([most] + holding)


def uneven_parts(stream_key, number_of, total, limit, slope):
    if number_of == 2:
        one = jax.random.randint(stream_key, (), max(1, total - limit), min(limit, total - 1) + 1)
        return jnp.stack([one, total - one])
    tallies = jnp.asarray(length_profile(number_of, total, limit, slope), jnp.int32)
    pairs = (number_of - 1) // 2
    giver, receiver = tallies[1:1 + 2 * pairs:2], tallies[2:2 + 2 * pairs:2]
    room = jnp.minimum(giver - 1, limit - receiver)
    shifted = jax.random.randint(jax.random.fold_in(stream_key, 1), (pairs,), 0, 1 << 20) % (room + 1)
    tallies = tallies.at[1:1 + 2 * pairs:2].set(giver - shifted).at[2:2 + 2 * pairs:2].set(receiver + shifted)
    return tallies[jax.random.permutation(jax.random.fold_in(stream_key, 2), number_of)]


def scatter_about(key, shape, width, most, shards=(), kind=jnp.bfloat16):
    result = jax.random.normal(key, shape, jnp.float32) * width
    if len(shards) > 0:
        result = block_levels(key, shape, shards, -0.22, 0.18) * result
    return jnp.clip(result, min=-most, max=most).astype(kind)


def setup_inputs(seed: int = 0) -> dict:
    seeds = jax.random.split(jax.random.key(seed), 6)
    query_rows = jnp.clip(jax.random.uniform(seeds[0], (TOKENS, HEADS * HEAD_DIM), jnp.float32, -2.0, 2.0) * block_levels(seeds[0], (TOKENS, HEADS * HEAD_DIM), ((0, 256),), -0.4, 0.0), -2.0, 2.0).astype(jnp.bfloat16)
    key_rows = jnp.clip(jax.random.uniform(seeds[1], (TOKENS, KV_HEADS * HEAD_DIM), jnp.float32, -2.0, 2.0) * block_levels(seeds[1], (TOKENS, KV_HEADS * HEAD_DIM), ((0, 256),), -0.4, 0.0), -2.0, 2.0).astype(jnp.bfloat16)
    value_rows = scatter_about(seeds[2], (TOKENS, KV_HEADS * HEAD_DIM), 1.0, 6.0, ((0, 256),))
    doc_ids = jnp.searchsorted(jnp.cumsum(uneven_parts(seeds[3], DOCS, NBLK, DOC_BLOCKS, 2)), jnp.arange(NBLK), side="right").astype(jnp.int32)
    grad_out = scatter_about(seeds[4], (TOKENS, HEADS * HEAD_DIM), 1.0, 6.0, ((0, 256),))
    return dict(query_rows=query_rows, key_rows=key_rows, value_rows=value_rows, doc_ids=doc_ids, grad_out=grad_out)


def rounded(values_in):
    return lax.optimization_barrier(values_in.astype(jnp.bfloat16)).astype(jnp.float32)


def reference(query_rows, key_rows, value_rows, doc_ids, grad_out):
    group_size = HEADS // KV_HEADS
    scaling = HEAD_DIM ** -0.5
    total_rows = query_rows.shape[0]
    margin = (WINDOW - 1) * TOK_DEV
    span_rows = WINDOW * TOK_DEV
    padded_keys = jnp.pad(key_rows, ((margin, 0), (0, 0)))
    padded_values = jnp.pad(value_rows, ((margin, 0), (0, 0)))
    positions = jnp.arange(total_rows, dtype=jnp.int32)
    token_docs = doc_ids[positions // BLOCK]
    padded_docs = jnp.concatenate([jnp.full((margin,), -1, jnp.int32), token_docs])
    padded_pos = jnp.arange(total_rows + margin, dtype=jnp.int32) - margin

    def one_block(carried, block_index):
        key_grads, value_grads = carried
        row_start = (block_index * TOK_DEV).astype(jnp.int32)
        block_queries = lax.dynamic_slice_in_dim(query_rows, row_start, TOK_DEV).astype(jnp.float32).reshape(TOK_DEV, KV_HEADS, group_size, HEAD_DIM)
        block_grads = lax.dynamic_slice_in_dim(grad_out, row_start, TOK_DEV).astype(jnp.float32).reshape(TOK_DEV, KV_HEADS, group_size, HEAD_DIM)
        query_docs = lax.dynamic_slice_in_dim(token_docs, row_start, TOK_DEV)
        query_pos = row_start + jnp.arange(TOK_DEV, dtype=jnp.int32)
        window_keys = lax.dynamic_slice_in_dim(padded_keys, row_start, span_rows).astype(jnp.float32).reshape(span_rows, KV_HEADS, HEAD_DIM)
        window_values = lax.dynamic_slice_in_dim(padded_values, row_start, span_rows).astype(jnp.float32).reshape(span_rows, KV_HEADS, HEAD_DIM)
        window_docs = lax.dynamic_slice_in_dim(padded_docs, row_start, span_rows)
        window_pos = lax.dynamic_slice_in_dim(padded_pos, row_start, span_rows)
        allowed = (query_docs[:, None] == window_docs[None, :]) & (window_pos[None, :] <= query_pos[:, None])
        scores = jnp.einsum("tkgd,skd->kgts", block_queries, window_keys) * scaling
        weights = jnp.where(allowed, jnp.exp(scores), 0.0)
        totals = jnp.sum(weights, axis=-1)
        weighted = jnp.einsum("kgts,skd->tkgd", rounded(weights), window_values)
        attention = lax.optimization_barrier((weighted / jnp.transpose(totals, (2, 0, 1))[..., None]).astype(jnp.bfloat16))
        log_totals = jnp.log(totals)
        out_dot = jnp.transpose(jnp.sum(block_grads * attention.astype(jnp.float32), axis=-1), (1, 2, 0))
        soft_probs = jnp.where(allowed, jnp.exp(scores - log_totals[..., None]), 0.0)
        grad_probs = jnp.einsum("tkgd,skd->kgts", block_grads, window_values)
        grad_scores = rounded(soft_probs * (grad_probs - out_dot[..., None]))
        grad_query = jnp.einsum("kgts,skd->tkgd", grad_scores, window_keys) * scaling
        grad_key = jnp.einsum("kgts,tkgd->skd", grad_scores, block_queries) * scaling
        grad_value = jnp.einsum("kgts,tkgd->skd", rounded(soft_probs), block_grads)
        key_grads = lax.dynamic_update_slice_in_dim(key_grads, lax.dynamic_slice_in_dim(key_grads, row_start, span_rows) + grad_key.reshape(span_rows, -1), row_start, 0)
        value_grads = lax.dynamic_update_slice_in_dim(value_grads, lax.dynamic_slice_in_dim(value_grads, row_start, span_rows) + grad_value.reshape(span_rows, -1), row_start, 0)
        return (key_grads, value_grads), (attention.reshape(TOK_DEV, -1), grad_query.reshape(TOK_DEV, -1))

    initial = (jnp.zeros((total_rows + margin, KV_HEADS * HEAD_DIM), jnp.float32), jnp.zeros((total_rows + margin, KV_HEADS * HEAD_DIM), jnp.float32))
    finals, stacked = lax.scan(one_block, initial, jnp.arange(N_CTX, dtype=jnp.int32))
    attention = stacked[0].reshape(total_rows, -1)
    grad_queries = stacked[1].reshape(total_rows, -1)
    return attention, grad_queries, finals[0][margin:], finals[1][margin:]
```

```python
import functools
import jax
import jax.numpy as jnp
from jax import lax
from jax.experimental import pallas as pl
from jax.experimental.pallas import tpu as pltpu
from jax.sharding import PartitionSpec as P

HEAD_DIM = 128
BLOCK = 128
NX = 4
MESH = pl.DeviceIdType.MESH
LOG2E = 1.4426950408889634
NEG = -1e30
F32 = jnp.float32
BF16 = jnp.bfloat16
NT = (((1,), (1,)), ((), ()))
NN = (((1,), (0,)), ((), ()))


def dot(a, b, dims=NN):
    return lax.dot_general(a, b, dims, preferred_element_type=F32)


def kernel(rows_n, tp_n, group, tok, docs, q_in, k_in, v_in, g_in,
           attn_out, dq_out, dk_out, dv_out,
           qh, gh, kvs, cbuf, kt, vt, bias, wts, inv_t, odot,
           attn_b, dqt, dq_b, dacc, dsend, r_m, r_b, y_b, y_c, ry1, ry2, own_b,
           land_a, land_q, land_k,
           kv_s, kv_r, q_s, q_r, g_s, g_r, loc,
           xm_s, xm_r, xb_s, xb_r, y_s, y_r,
           dm_s, dm_r, db_s, db_r, dy_s, dy_r,
           oa_s, oa_r, oq_s, oq_r, ok_s, ok_r):
    stretch = rows_n_tokens = kvs.shape[2]
    scale = HEAD_DIM ** -0.5
    gw = group * HEAD_DIM
    c = lax.axis_index("ctx")
    p = lax.axis_index("tp")
    row = c // NX
    x = lax.rem(c, NX)

    def tp_at(i):
        return lax.rem(p + i, tp_n)

    def mate_x(i):
        return lax.rem(x + i, NX)

    def ctx_at(r, xx):
        return r * NX + xx

    def rcopy(src, dst, ss, rs, dev):
        return pltpu.make_async_remote_copy(
            src_ref=src, dst_ref=dst, send_sem=ss, recv_sem=rs, device_id=dev, device_id_type=MESH)

    barrier = pltpu.get_barrier_semaphore()
    for i in range(1, tp_n):
        pl.semaphore_signal(barrier, inc=1, device_id={"ctx": c, "tp": tp_at(i)}, device_id_type=MESH)
    for i in range(1, NX):
        pl.semaphore_signal(barrier, inc=1, device_id={"ctx": ctx_at(row, mate_x(i)), "tp": p}, device_id_type=MESH)
    for k in (1, 2, rows_n - 1, rows_n - 2):
        pl.semaphore_signal(
            barrier, inc=1, device_id={"ctx": ctx_at(lax.rem(row + k, rows_n), x), "tp": p}, device_id_type=MESH)
    pl.semaphore_wait(barrier, tp_n - 1 + NX - 1 + 4)

    my_rows = pl.ds(pl.multiple_of(p * tok, tok), tok)

    def cols(t, w):
        return pl.ds(pl.multiple_of(t * w, w), w)

    kv_copies = []
    for i in range(1, tp_n):
        t = tp_at(i)
        for n, src in ((0, k_in), (1, v_in)):
            cp = rcopy(src.at[:, cols(t, HEAD_DIM)], kvs.at[x, n, my_rows, :], kv_s.at[n, i - 1], kv_r.at[n, i - 1],
                       {"ctx": c, "tp": t})
            cp.start()
            kv_copies.append(cp)
    locals_ = [
        pltpu.make_async_copy(k_in.at[:, cols(p, HEAD_DIM)], kvs.at[x, 0, my_rows, :], loc.at[0]),
        pltpu.make_async_copy(v_in.at[:, cols(p, HEAD_DIM)], kvs.at[x, 1, my_rows, :], loc.at[1]),
        pltpu.make_async_copy(q_in.at[:, cols(p, gw)], qh.at[my_rows, :], loc.at[2]),
        pltpu.make_async_copy(g_in.at[:, cols(p, gw)], gh.at[my_rows, :], loc.at[3]),
    ]
    for cp in locals_:
        cp.start()
    q_copies = []
    for i in range(1, tp_n):
        t = tp_at(i)
        cp = rcopy(q_in.at[:, cols(t, gw)], qh.at[my_rows, :], q_s.at[i - 1], q_r.at[i - 1], {"ctx": c, "tp": t})
        cp.start()
        q_copies.append(cp)

    @pl.when(row < 2)
    def _():
        for i in range(1, NX):
            @pl.when(mate_x(i) > x)
            def _():
                kvs[mate_x(i)] = jnp.zeros(kvs.shape[1:], BF16)

    @pl.when(row < 1)
    def _():
        kvs[NX:] = jnp.zeros((NX,) + kvs.shape[1:], BF16)

    lane = lax.broadcasted_iota(jnp.int32, (1, stretch), 1)
    per = stretch // BLOCK
    q_doc = [docs[c * per + b] for b in range(per)]
    for slot in range(2 * NX):
        xs = slot % NX
        if slot < NX:
            src = jnp.where(xs <= x, c - x + xs, c - x + xs - 2 * NX)
        else:
            src = c - x + xs - NX
        own = (src == c).astype(jnp.int32)
        for b in range(per):
            k_doc = jnp.where(src >= 0, docs[jnp.maximum(src, 0) * per + b], -1)
            line = jnp.where(lane < BLOCK, jnp.where(k_doc == q_doc[0], 0.0, NEG), jnp.where(k_doc == q_doc[1], 0.0, NEG))
            key_at = lax.broadcasted_iota(jnp.int32, (BLOCK, stretch), 0) + b * BLOCK
            q_at = lax.broadcasted_iota(jnp.int32, (BLOCK, stretch), 1)
            late = (key_at - q_at) * own > 0
            bias[slot, b * BLOCK:(b + 1) * BLOCK, :] = jnp.where(late, NEG, jnp.broadcast_to(line, (BLOCK, stretch)))

    locals_[0].wait()
    locals_[1].wait()
    for cp in kv_copies:
        cp.wait_recv()

    def x_own(i):
        return rcopy(kvs.at[x], kvs.at[x], xm_s.at[i - 1], xm_r.at[i - 1], {"ctx": ctx_at(row, mate_x(i)), "tp": p})

    def x_far(i):
        return rcopy(cbuf, kvs.at[x], xm_s.at[i - 1], xm_r.at[i - 1], {"ctx": ctx_at(row, mate_x(i)), "tp": p})

    def x_prev(i):
        return rcopy(kvs.at[NX + x], kvs.at[NX + x], xb_s.at[i - 1], xb_r.at[i - 1],
                     {"ctx": ctx_at(row, mate_x(i)), "tp": p})

    to_next = rcopy(kvs.at[x], kvs.at[NX + x], y_s.at[0], y_r.at[0], {"ctx": c + NX, "tp": p})
    to_second = rcopy(kvs.at[x], cbuf, y_s.at[1], y_r.at[1], {"ctx": c + 2 * NX, "tp": p})
    has_next = row + 1 < rows_n
    has_second = (row + 2 < rows_n) & (x > 0)
    from_prev = row >= 1
    from_second = (row >= 2) & (x > 0)

    @pl.when(has_next)
    def _():
        to_next.start()

    @pl.when(has_second)
    def _():
        to_second.start()

    for i in range(1, NX):
        @pl.when(mate_x(i) > x)
        def _():
            x_own(i).start()

    g_copies = []
    for i in range(1, tp_n):
        t = tp_at(i)
        cp = rcopy(g_in.at[:, cols(t, gw)], gh.at[my_rows, :], g_s.at[i - 1], g_r.at[i - 1], {"ctx": c, "tp": t})
        cp.start()
        g_copies.append(cp)

    @pl.when(from_prev)
    def _():
        to_next.wait_recv()
        for i in range(1, NX):
            x_prev(i).start()

    @pl.when(from_second)
    def _():
        to_second.wait_recv()
        for i in range(1, NX):
            @pl.when(mate_x(i) < x)
            def _():
                x_far(i).start()

    for i in range(1, NX):
        @pl.when((lax.rem(x + NX - i, NX) < x) | (row >= 2))
        def _():
            x_own(i).wait_recv()

    @pl.when(from_prev)
    def _():
        for i in range(1, NX):
            x_prev(i).wait_recv()

    for slot in range(2 * NX):
        kt[:, slot * stretch:(slot + 1) * stretch] = jnp.transpose(kvs[slot, 0].astype(F32)).astype(BF16)
        vt[:, slot * stretch:(slot + 1) * stretch] = jnp.transpose(kvs[slot, 1].astype(F32)).astype(BF16)

    locals_[2].wait()
    for cp in q_copies:
        cp.wait_recv()

    def forward(h, carry):
        at = pl.ds(pl.multiple_of(h * HEAD_DIM, HEAD_DIM), HEAD_DIM)
        q = qh[:, at]
        total = jnp.zeros((1, stretch), F32)
        out_t = jnp.zeros((HEAD_DIM, stretch), F32)
        for slot in range(2 * NX):
            s = dot(kvs[slot, 0], q, NT)
            w = jnp.exp2(s * (scale * LOG2E) + bias[slot])
            wts[h, slot] = w
            total = total + jnp.sum(w, axis=0, keepdims=True)
            out_t = out_t + dot(vt[:, slot * stretch:(slot + 1) * stretch], w.astype(BF16))
        inv_t[h] = 1.0 / total
        attn_b[:, at] = jnp.transpose(out_t / total).astype(BF16)
        return carry

    lax.fori_loop(0, group, forward, 0)

    a_copies = []
    for i in range(1, tp_n):
        t = tp_at(i)
        cp = rcopy(attn_b.at[cols(t, tok), :], land_a.at[:, cols(p, gw)], oa_s.at[i - 1], oa_r.at[i - 1],
                   {"ctx": c, "tp": t})
        cp.start()
        a_copies.append(cp)

    locals_[3].wait()
    for cp in g_copies:
        cp.wait_recv()

    def dots(h, carry):
        at = pl.ds(pl.multiple_of(h * HEAD_DIM, HEAD_DIM), HEAD_DIM)
        prod = gh[:, at].astype(F32) * attn_b[:, at].astype(F32)
        odot[h] = jnp.sum(jnp.transpose(prod), axis=0, keepdims=True)
        dqt[h] = jnp.zeros((HEAD_DIM, stretch), F32)
        return carry

    lax.fori_loop(0, group, dots, 0)

    def d_m(i):
        return rcopy(dsend.at[mate_x(i)], r_m.at[i - 1], dm_s.at[i - 1], dm_r.at[i - 1],
                     {"ctx": ctx_at(row, mate_x(i)), "tp": p})

    def d_b(i):
        return rcopy(dsend.at[NX + mate_x(i)], r_b.at[i - 1], db_s.at[i - 1], db_r.at[i - 1],
                     {"ctx": ctx_at(row, mate_x(i)), "tp": p})

    def backward(slot):
        dacc[...] = jnp.zeros_like(dacc)
        k_t = kt[:, pl.ds(pl.multiple_of(slot * stretch, stretch), stretch)]

        def head(h, carry):
            at = pl.ds(pl.multiple_of(h * HEAD_DIM, HEAD_DIM), HEAD_DIM)
            q = qh[:, at]
            g = gh[:, at]
            pr = wts[h, slot] * inv_t[h]
            dp = dot(kvs[slot, 1], g, NT)
            ds = (pr * (dp - odot[h])).astype(BF16)
            dacc[1] += dot(pr.astype(BF16), g)
            dacc[0] += dot(ds, q)
            dqt[h] += dot(k_t, ds)
            return carry

        lax.fori_loop(0, group, head, 0)

    for i in (1, 2, 3, 0):
        slot = NX + mate_x(i)
        backward(slot)
        dsend[slot, 0] = (dacc[0] * scale).astype(BF16)
        dsend[slot, 1] = dacc[1].astype(BF16)
        if i:
            d_b(i).start()
    for i in (1, 2, 3, 0):
        slot = mate_x(i)
        backward(slot)
        if i:
            dsend[slot, 0] = (dacc[0] * scale).astype(BF16)
            dsend[slot, 1] = dacc[1].astype(BF16)
            d_m(i).start()

    for h in range(group):
        dq_b[:, h * HEAD_DIM:(h + 1) * HEAD_DIM] = (jnp.transpose(dqt[h]) * scale).astype(BF16)
    dq_copies = []
    for i in range(1, tp_n):
        t = tp_at(i)
        cp = rcopy(dq_b.at[cols(t, tok), :], land_q.at[:, cols(p, gw)], oq_s.at[i - 1], oq_r.at[i - 1],
                   {"ctx": c, "tp": t})
        cp.start()
        dq_copies.append(cp)

    for i in range(1, NX):
        d_b(i).wait_recv()
    y_b[...] = (dsend[NX + x].astype(F32) + r_b[0].astype(F32) + r_b[1].astype(F32) + r_b[2].astype(F32)).astype(BF16)
    back_one = rcopy(y_b, ry1, dy_s.at[0], dy_r.at[0], {"ctx": c - NX, "tp": p})
    back_two = rcopy(y_c, ry2, dy_s.at[1], dy_r.at[1], {"ctx": c - 2 * NX, "tp": p})

    @pl.when(from_prev)
    def _():
        back_one.start()

    for i in range(1, NX):
        d_m(i).wait_recv()
    dacc[0] = dacc[0] * scale
    far = jnp.zeros(dacc.shape, F32)
    near = dacc[...]
    for i in range(1, NX):
        xs = lax.rem(x + NX - i, NX)
        got = r_m[i - 1].astype(F32)
        far = far + jnp.where(xs < x, got, 0.0)
        near = near + jnp.where(xs > x, got, 0.0)
    y_c[...] = far.astype(BF16)
    dacc[...] = near

    @pl.when(from_second)
    def _():
        back_two.start()

    @pl.when(has_next)
    def _():
        back_one.wait_recv()
        dacc[...] += ry1[...].astype(F32)

    @pl.when(has_second)
    def _():
        back_two.wait_recv()
        dacc[...] += ry2[...].astype(F32)

    own_b[...] = dacc[...].astype(BF16)
    k_copies = []
    for i in range(1, tp_n):
        t = tp_at(i)
        cp = rcopy(own_b.at[:, cols(t, tok), :], land_k.at[:, :, cols(p, HEAD_DIM)], ok_s.at[i - 1], ok_r.at[i - 1],
                   {"ctx": c, "tp": t})
        cp.start()
        k_copies.append(cp)

    land_a[:, cols(p, gw)] = attn_b[my_rows, :]
    land_q[:, cols(p, gw)] = dq_b[my_rows, :]
    land_k[:, :, cols(p, HEAD_DIM)] = own_b[:, my_rows, :]
    for cp in a_copies:
        cp.wait_recv()
    attn_out[...] = land_a[...]
    for cp in dq_copies:
        cp.wait_recv()
    dq_out[...] = land_q[...].astype(F32)
    for cp in k_copies:
        cp.wait_recv()
    dk_out[...] = land_k[0].astype(F32)
    dv_out[...] = land_k[1].astype(F32)

    for cp in kv_copies + q_copies + g_copies + a_copies + dq_copies + k_copies:
        cp.wait_send()
    for i in range(1, NX):
        @pl.when((mate_x(i) > x) | (row >= 2))
        def _():
            x_own(i).wait_send()
        d_m(i).wait_send()
        d_b(i).wait_send()

    @pl.when(from_prev)
    def _():
        for i in range(1, NX):
            x_prev(i).wait_send()
        back_one.wait_send()

    @pl.when(from_second)
    def _():
        back_two.wait_send()

    @pl.when(has_next)
    def _():
        to_next.wait_send()

    @pl.when(has_second)
    def _():
        to_second.wait_send()


def solution(mesh):
    ctx_n, tp_n = mesh.shape["ctx"], mesh.shape["tp"]
    rows_n = ctx_n // NX

    def local(query_rows, key_rows, value_rows, doc_ids, grad_out):
        tok, width = query_rows.shape
        kw = key_rows.shape[1]
        stretch = tok * tp_n
        gw = width // tp_n
        group = gw // HEAD_DIM
        n2 = 2 * NX
        dma = pltpu.SemaphoreType.DMA
        piece = (2, stretch, HEAD_DIM)
        V = pltpu.VMEM
        anyspec = pl.BlockSpec(memory_space=pl.ANY)
        vspec = pl.BlockSpec(memory_space=pltpu.VMEM)
        scratch = [
            V((stretch, gw), BF16), V((stretch, gw), BF16), V((n2,) + piece, BF16), V(piece, BF16),
            V((HEAD_DIM, n2 * stretch), BF16), V((HEAD_DIM, n2 * stretch), BF16), V((n2, stretch, stretch), F32),
            V((group, n2, stretch, stretch), F32), V((group, 1, stretch), F32), V((group, 1, stretch), F32),
            V((stretch, gw), BF16), V((group, HEAD_DIM, stretch), F32), V((stretch, gw), BF16),
            V(piece, F32), V((n2,) + piece, BF16), V((NX - 1,) + piece, BF16), V((NX - 1,) + piece, BF16),
            V(piece, BF16), V(piece, BF16), V(piece, BF16), V(piece, BF16), V(piece, BF16),
            V((tok, width), BF16), V((tok, width), BF16), V((2, tok, kw), BF16),
            dma((2, tp_n - 1)), dma((2, tp_n - 1)), dma((tp_n - 1,)), dma((tp_n - 1,)), dma((tp_n - 1,)),
            dma((tp_n - 1,)), dma((4,)),
            dma((NX - 1,)), dma((NX - 1,)), dma((NX - 1,)), dma((NX - 1,)), dma((2,)), dma((2,)),
            dma((NX - 1,)), dma((NX - 1,)), dma((NX - 1,)), dma((NX - 1,)), dma((2,)), dma((2,)),
            dma((tp_n - 1,)), dma((tp_n - 1,)), dma((tp_n - 1,)), dma((tp_n - 1,)), dma((tp_n - 1,)), dma((tp_n - 1,)),
        ]
        return pl.pallas_call(
            functools.partial(kernel, rows_n, tp_n, group, tok),
            out_shape=(
                jax.ShapeDtypeStruct((tok, width), BF16),
                jax.ShapeDtypeStruct((tok, width), F32),
                jax.ShapeDtypeStruct((tok, kw), F32),
                jax.ShapeDtypeStruct((tok, kw), F32),
            ),
            in_specs=[pl.BlockSpec(memory_space=pltpu.SMEM)] + [anyspec] * 4,
            out_specs=(vspec,) * 4,
            scratch_shapes=scratch,
            compiler_params=pltpu.CompilerParams(
                collective_id=0, has_side_effects=True, vmem_limit_bytes=60 * 1024 * 1024),
            name="attention_layer",
        )(doc_ids, query_rows, key_rows, value_rows, grad_out)

    rows = P(("ctx", "tp"), None)
    return jax.shard_map(
        local, mesh=mesh, in_specs=(rows, rows, rows, P(), rows), out_specs=(rows,) * 4, check_vma=False)
```

```python
import functools
import jax
import jax.numpy as jnp
from jax import lax
from jax.experimental import pallas as pl
from jax.experimental.pallas import tpu as pltpu
from jax.sharding import PartitionSpec as P

HEAD_DIM = 128
BLOCK = 128
NX = 4
MESH = pl.DeviceIdType.MESH
LOG2E = 1.4426950408889634
NEG = -1e30
F32 = jnp.float32
BF16 = jnp.bfloat16
NT = (((1,), (1,)), ((), ()))
NN = (((1,), (0,)), ((), ()))


def dot(a, b, dims=NN):
    return lax.dot_general(a, b, dims, preferred_element_type=F32)


def kernel(rows_n, tp_n, group, tok, docs, q_in, k_in, v_in, g_in,
           attn_out, dq_out, dk_out, dv_out,
           qh, gh, kvs, cbuf, kt, vt, bias, wts, inv_t, odot,
           attn_b, dqt, dq_b, dacc, dsend, r_m, r_b, y_b, y_c, ry1, ry2, own_b,
           land_a, land_q, land_k,
           kv_s, kv_r, q_s, q_r, g_s, g_r, loc,
           xm_s, xm_r, xb_s, xb_r, y_s, y_r,
           dm_s, dm_r, db_s, db_r, dy_s, dy_r,
           oa_s, oa_r, oq_s, oq_r, ok_s, ok_r):
    stretch = rows_n_tokens = kvs.shape[2]
    scale = HEAD_DIM ** -0.5
    gw = group * HEAD_DIM
    c = lax.axis_index("ctx")
    p = lax.axis_index("tp")
    row = c // NX
    x = lax.rem(c, NX)

    def tp_at(i):
        return lax.rem(p + i, tp_n)

    def flip(r, t):
        return t + lax.rem(r // (rows_n // 2), 2) * (tp_n - 2 - 4 * (t // 2))

    def head_at(t):
        return flip(row, t)

    me = head_at(p)

    def mate_x(i):
        return lax.rem(x + i, NX)

    def ctx_at(r, xx):
        return r * NX + xx

    def row_at(k):
        return {"ctx": c + k * NX, "tp": flip(row + k, me)}

    def rcopy(src, dst, ss, rs, dev):
        return pltpu.make_async_remote_copy(
            src_ref=src, dst_ref=dst, send_sem=ss, recv_sem=rs, device_id=dev, device_id_type=MESH)

    barrier = pltpu.get_barrier_semaphore()
    for i in range(1, tp_n):
        pl.semaphore_signal(barrier, inc=1, device_id={"ctx": c, "tp": tp_at(i)}, device_id_type=MESH)
    for i in range(1, NX):
        pl.semaphore_signal(barrier, inc=1, device_id={"ctx": ctx_at(row, mate_x(i)), "tp": p}, device_id_type=MESH)
    for k in (1, 2, rows_n - 1, rows_n - 2):
        r = lax.rem(row + k, rows_n)
        pl.semaphore_signal(
            barrier, inc=1, device_id={"ctx": ctx_at(r, x), "tp": flip(r, me)}, device_id_type=MESH)
    pl.semaphore_wait(barrier, tp_n - 1 + NX - 1 + 4)

    my_rows = pl.ds(pl.multiple_of(p * tok, tok), tok)

    def cols(t, w):
        return pl.ds(pl.multiple_of(t * w, w), w)

    kv_copies = []
    for i in range(1, tp_n):
        t = tp_at(i)
        for n, src in ((0, k_in), (1, v_in)):
            cp = rcopy(src.at[:, cols(head_at(t), HEAD_DIM)], kvs.at[x, n, my_rows, :], kv_s.at[n, i - 1], kv_r.at[n, i - 1],
                       {"ctx": c, "tp": t})
            cp.start()
            kv_copies.append(cp)
    locals_ = [
        pltpu.make_async_copy(k_in.at[:, cols(me, HEAD_DIM)], kvs.at[x, 0, my_rows, :], loc.at[0]),
        pltpu.make_async_copy(v_in.at[:, cols(me, HEAD_DIM)], kvs.at[x, 1, my_rows, :], loc.at[1]),
        pltpu.make_async_copy(q_in.at[:, cols(me, gw)], qh.at[my_rows, :], loc.at[2]),
        pltpu.make_async_copy(g_in.at[:, cols(me, gw)], gh.at[my_rows, :], loc.at[3]),
    ]
    for cp in locals_:
        cp.start()
    q_copies = []
    for i in range(1, tp_n):
        t = tp_at(i)
        cp = rcopy(q_in.at[:, cols(head_at(t), gw)], qh.at[my_rows, :], q_s.at[i - 1], q_r.at[i - 1], {"ctx": c, "tp": t})
        cp.start()
        q_copies.append(cp)

    @pl.when(row < 2)
    def _():
        for i in range(1, NX):
            @pl.when(mate_x(i) > x)
            def _():
                kvs[mate_x(i)] = jnp.zeros(kvs.shape[1:], BF16)

    @pl.when(row < 1)
    def _():
        kvs[NX:] = jnp.zeros((NX,) + kvs.shape[1:], BF16)

    lane = lax.broadcasted_iota(jnp.int32, (1, stretch), 1)
    per = stretch // BLOCK
    q_doc = [docs[c * per + b] for b in range(per)]
    for slot in range(2 * NX):
        xs = slot % NX
        if slot < NX:
            src = jnp.where(xs <= x, c - x + xs, c - x + xs - 2 * NX)
        else:
            src = c - x + xs - NX
        own = (src == c).astype(jnp.int32)
        for b in range(per):
            k_doc = jnp.where(src >= 0, docs[jnp.maximum(src, 0) * per + b], -1)
            line = jnp.where(lane < BLOCK, jnp.where(k_doc == q_doc[0], 0.0, NEG), jnp.where(k_doc == q_doc[1], 0.0, NEG))
            key_at = lax.broadcasted_iota(jnp.int32, (BLOCK, stretch), 0) + b * BLOCK
            q_at = lax.broadcasted_iota(jnp.int32, (BLOCK, stretch), 1)
            late = (key_at - q_at) * own > 0
            bias[slot, b * BLOCK:(b + 1) * BLOCK, :] = jnp.where(late, NEG, jnp.broadcast_to(line, (BLOCK, stretch)))

    locals_[0].wait()
    locals_[1].wait()
    for cp in kv_copies:
        cp.wait_recv()

    def x_own(i):
        return rcopy(kvs.at[x], kvs.at[x], xm_s.at[i - 1], xm_r.at[i - 1], {"ctx": ctx_at(row, mate_x(i)), "tp": p})

    def x_far(i):
        return rcopy(cbuf, kvs.at[x], xm_s.at[i - 1], xm_r.at[i - 1], {"ctx": ctx_at(row, mate_x(i)), "tp": p})

    def x_prev(i):
        return rcopy(kvs.at[NX + x], kvs.at[NX + x], xb_s.at[i - 1], xb_r.at[i - 1],
                     {"ctx": ctx_at(row, mate_x(i)), "tp": p})

    to_next = rcopy(kvs.at[x], kvs.at[NX + x], y_s.at[0], y_r.at[0], row_at(1))
    to_second = rcopy(kvs.at[x], cbuf, y_s.at[1], y_r.at[1], row_at(2))
    has_next = row + 1 < rows_n
    has_second = (row + 2 < rows_n) & (x > 0)
    from_prev = row >= 1
    from_second = (row >= 2) & (x > 0)

    @pl.when(has_next)
    def _():
        to_next.start()

    @pl.when(has_second)
    def _():
        to_second.start()

    for i in range(1, NX):
        @pl.when(mate_x(i) > x)
        def _():
            x_own(i).start()

    g_copies = []
    for i in range(1, tp_n):
        t = tp_at(i)
        cp = rcopy(g_in.at[:, cols(head_at(t), gw)], gh.at[my_rows, :], g_s.at[i - 1], g_r.at[i - 1], {"ctx": c, "tp": t})
        cp.start()
        g_copies.append(cp)

    @pl.when(from_prev)
    def _():
        to_next.wait_recv()
        for i in range(1, NX):
            x_prev(i).start()

    @pl.when(from_second)
    def _():
        to_second.wait_recv()
        for i in range(1, NX):
            @pl.when(mate_x(i) < x)
            def _():
                x_far(i).start()

    for i in range(1, NX):
        @pl.when((lax.rem(x + NX - i, NX) < x) | (row >= 2))
        def _():
            x_own(i).wait_recv()

    @pl.when(from_prev)
    def _():
        for i in range(1, NX):
            x_prev(i).wait_recv()

    for slot in range(2 * NX):
        kt[:, slot * stretch:(slot + 1) * stretch] = jnp.transpose(kvs[slot, 0].astype(F32)).astype(BF16)
        vt[:, slot * stretch:(slot + 1) * stretch] = jnp.transpose(kvs[slot, 1].astype(F32)).astype(BF16)

    locals_[2].wait()
    for cp in q_copies:
        cp.wait_recv()

    def forward(h, carry):
        at = pl.ds(pl.multiple_of(h * HEAD_DIM, HEAD_DIM), HEAD_DIM)
        q = qh[:, at]
        total = jnp.zeros((1, stretch), F32)
        out_t = jnp.zeros((HEAD_DIM, stretch), F32)
        for slot in range(2 * NX):
            s = dot(kvs[slot, 0], q, NT)
            w = jnp.exp2(s * (scale * LOG2E) + bias[slot])
            wts[h, slot] = w
            total = total + jnp.sum(w, axis=0, keepdims=True)
            out_t = out_t + dot(vt[:, slot * stretch:(slot + 1) * stretch], w.astype(BF16))
        inv_t[h] = 1.0 / total
        attn_b[:, at] = jnp.transpose(out_t / total).astype(BF16)
        return carry

    lax.fori_loop(0, group, forward, 0)

    a_copies = []
    for i in range(1, tp_n):
        t = tp_at(i)
        cp = rcopy(attn_b.at[cols(t, tok), :], land_a.at[:, cols(me, gw)], oa_s.at[i - 1], oa_r.at[i - 1],
                   {"ctx": c, "tp": t})
        cp.start()
        a_copies.append(cp)

    locals_[3].wait()
    for cp in g_copies:
        cp.wait_recv()

    def dots(h, carry):
        at = pl.ds(pl.multiple_of(h * HEAD_DIM, HEAD_DIM), HEAD_DIM)
        prod = gh[:, at].astype(F32) * attn_b[:, at].astype(F32)
        odot[h] = jnp.sum(jnp.transpose(prod), axis=0, keepdims=True)
        dqt[h] = jnp.zeros((HEAD_DIM, stretch), F32)
        return carry

    lax.fori_loop(0, group, dots, 0)

    def d_m(i):
        return rcopy(dsend.at[mate_x(i)], r_m.at[i - 1], dm_s.at[i - 1], dm_r.at[i - 1],
                     {"ctx": ctx_at(row, mate_x(i)), "tp": p})

    def d_b(i):
        return rcopy(dsend.at[NX + mate_x(i)], r_b.at[i - 1], db_s.at[i - 1], db_r.at[i - 1],
                     {"ctx": ctx_at(row, mate_x(i)), "tp": p})

    def backward(slot):
        dacc[...] = jnp.zeros_like(dacc)
        k_t = kt[:, pl.ds(pl.multiple_of(slot * stretch, stretch), stretch)]

        def head(h, carry):
            at = pl.ds(pl.multiple_of(h * HEAD_DIM, HEAD_DIM), HEAD_DIM)
            q = qh[:, at]
            g = gh[:, at]
            pr = wts[h, slot] * inv_t[h]
            dp = dot(kvs[slot, 1], g, NT)
            ds = (pr * (dp - odot[h])).astype(BF16)
            dacc[1] += dot(pr.astype(BF16), g)
            dacc[0] += dot(ds, q)
            dqt[h] += dot(k_t, ds)
            return carry

        lax.fori_loop(0, group, head, 0)

    for i in (1, 2, 3, 0):
        slot = NX + mate_x(i)
        backward(slot)
        dsend[slot, 0] = (dacc[0] * scale).astype(BF16)
        dsend[slot, 1] = dacc[1].astype(BF16)
        if i:
            d_b(i).start()
    for i in (1, 2, 3, 0):
        slot = mate_x(i)
        backward(slot)
        if i:
            dsend[slot, 0] = (dacc[0] * scale).astype(BF16)
            dsend[slot, 1] = dacc[1].astype(BF16)
            d_m(i).start()

    for h in range(group):
        dq_b[:, h * HEAD_DIM:(h + 1) * HEAD_DIM] = (jnp.transpose(dqt[h]) * scale).astype(BF16)
    dq_copies = []
    for i in range(1, tp_n):
        t = tp_at(i)
        cp = rcopy(dq_b.at[cols(t, tok), :], land_q.at[:, cols(me, gw)], oq_s.at[i - 1], oq_r.at[i - 1],
                   {"ctx": c, "tp": t})
        cp.start()
        dq_copies.append(cp)

    for i in range(1, NX):
        d_b(i).wait_recv()
    y_b[...] = (dsend[NX + x].astype(F32) + r_b[0].astype(F32) + r_b[1].astype(F32) + r_b[2].astype(F32)).astype(BF16)
    back_one = rcopy(y_b, ry1, dy_s.at[0], dy_r.at[0], row_at(-1))
    back_two = rcopy(y_c, ry2, dy_s.at[1], dy_r.at[1], row_at(-2))

    @pl.when(from_prev)
    def _():
        back_one.start()

    for i in range(1, NX):
        d_m(i).wait_recv()
    dacc[0] = dacc[0] * scale
    far = jnp.zeros(dacc.shape, F32)
    near = dacc[...]
    for i in range(1, NX):
        xs = lax.rem(x + NX - i, NX)
        got = r_m[i - 1].astype(F32)
        far = far + jnp.where(xs < x, got, 0.0)
        near = near + jnp.where(xs > x, got, 0.0)
    y_c[...] = far.astype(BF16)
    dacc[...] = near

    @pl.when(from_second)
    def _():
        back_two.start()

    @pl.when(has_next)
    def _():
        back_one.wait_recv()
        dacc[...] += ry1[...].astype(F32)

    @pl.when(has_second)
    def _():
        back_two.wait_recv()
        dacc[...] += ry2[...].astype(F32)

    own_b[...] = dacc[...].astype(BF16)
    k_copies = []
    for i in range(1, tp_n):
        t = tp_at(i)
        cp = rcopy(own_b.at[:, cols(t, tok), :], land_k.at[:, :, cols(me, HEAD_DIM)], ok_s.at[i - 1], ok_r.at[i - 1],
                   {"ctx": c, "tp": t})
        cp.start()
        k_copies.append(cp)

    land_a[:, cols(me, gw)] = attn_b[my_rows, :]
    land_q[:, cols(me, gw)] = dq_b[my_rows, :]
    land_k[:, :, cols(me, HEAD_DIM)] = own_b[:, my_rows, :]
    for cp in a_copies:
        cp.wait_recv()
    attn_out[...] = land_a[...]
    for cp in dq_copies:
        cp.wait_recv()
    dq_out[...] = land_q[...].astype(F32)
    for cp in k_copies:
        cp.wait_recv()
    dk_out[...] = land_k[0].astype(F32)
    dv_out[...] = land_k[1].astype(F32)

    for cp in kv_copies + q_copies + g_copies + a_copies + dq_copies + k_copies:
        cp.wait_send()
    for i in range(1, NX):
        @pl.when((mate_x(i) > x) | (row >= 2))
        def _():
            x_own(i).wait_send()
        d_m(i).wait_send()
        d_b(i).wait_send()

    @pl.when(from_prev)
    def _():
        for i in range(1, NX):
            x_prev(i).wait_send()
        back_one.wait_send()

    @pl.when(from_second)
    def _():
        back_two.wait_send()

    @pl.when(has_next)
    def _():
        to_next.wait_send()

    @pl.when(has_second)
    def _():
        to_second.wait_send()


def solution(mesh):
    ctx_n, tp_n = mesh.shape["ctx"], mesh.shape["tp"]
    rows_n = ctx_n // NX

    def local(query_rows, key_rows, value_rows, doc_ids, grad_out):
        tok, width = query_rows.shape
        kw = key_rows.shape[1]
        stretch = tok * tp_n
        gw = width // tp_n
        group = gw // HEAD_DIM
        n2 = 2 * NX
        dma = pltpu.SemaphoreType.DMA
        piece = (2, stretch, HEAD_DIM)
        V = pltpu.VMEM
        anyspec = pl.BlockSpec(memory_space=pl.ANY)
        vspec = pl.BlockSpec(memory_space=pltpu.VMEM)
        scratch = [
            V((stretch, gw), BF16), V((stretch, gw), BF16), V((n2,) + piece, BF16), V(piece, BF16),
            V((HEAD_DIM, n2 * stretch), BF16), V((HEAD_DIM, n2 * stretch), BF16), V((n2, stretch, stretch), F32),
            V((group, n2, stretch, stretch), F32), V((group, 1, stretch), F32), V((group, 1, stretch), F32),
            V((stretch, gw), BF16), V((group, HEAD_DIM, stretch), F32), V((stretch, gw), BF16),
            V(piece, F32), V((n2,) + piece, BF16), V((NX - 1,) + piece, BF16), V((NX - 1,) + piece, BF16),
            V(piece, BF16), V(piece, BF16), V(piece, BF16), V(piece, BF16), V(piece, BF16),
            V((tok, width), BF16), V((tok, width), BF16), V((2, tok, kw), BF16),
            dma((2, tp_n - 1)), dma((2, tp_n - 1)), dma((tp_n - 1,)), dma((tp_n - 1,)), dma((tp_n - 1,)),
            dma((tp_n - 1,)), dma((4,)),
            dma((NX - 1,)), dma((NX - 1,)), dma((NX - 1,)), dma((NX - 1,)), dma((2,)), dma((2,)),
            dma((NX - 1,)), dma((NX - 1,)), dma((NX - 1,)), dma((NX - 1,)), dma((2,)), dma((2,)),
            dma((tp_n - 1,)), dma((tp_n - 1,)), dma((tp_n - 1,)), dma((tp_n - 1,)), dma((tp_n - 1,)), dma((tp_n - 1,)),
        ]
        return pl.pallas_call(
            functools.partial(kernel, rows_n, tp_n, group, tok),
            out_shape=(
                jax.ShapeDtypeStruct((tok, width), BF16),
                jax.ShapeDtypeStruct((tok, width), F32),
                jax.ShapeDtypeStruct((tok, kw), F32),
                jax.ShapeDtypeStruct((tok, kw), F32),
            ),
            in_specs=[pl.BlockSpec(memory_space=pltpu.SMEM)] + [anyspec] * 4,
            out_specs=(vspec,) * 4,
            scratch_shapes=scratch,
            compiler_params=pltpu.CompilerParams(
                collective_id=0, has_side_effects=True, vmem_limit_bytes=60 * 1024 * 1024),
            name="attention_layer",
        )(doc_ids, query_rows, key_rows, value_rows, grad_out)

    rows = P(("ctx", "tp"), None)
    return jax.shard_map(
        local, mesh=mesh, in_specs=(rows, rows, rows, P(), rows), out_specs=(rows,) * 4, check_vma=False)
```

```python
import functools
import jax
import jax.numpy as jnp
from jax import lax
from jax.experimental import pallas as pl
from jax.experimental.pallas import tpu as pltpu
from jax.sharding import PartitionSpec as P

HEAD_DIM = 128
BLOCK = 128
NX = 4
MESH = pl.DeviceIdType.MESH
LOG2E = 1.4426950408889634
NEG = -1e30
F32 = jnp.float32
BF16 = jnp.bfloat16
NT = (((1,), (1,)), ((), ()))
NN = (((1,), (0,)), ((), ()))


def dot(a, b, dims=NN):
    return lax.dot_general(a, b, dims, preferred_element_type=F32)


def kernel(rows_n, tp_n, group, tok, docs, q_in, k_in, v_in, g_in,
           attn_out, dq_out, dkv_out,
           qh, gh, kvs, cbuf, kt, vt, bias, wts, inv_t, odot,
           attn_b, dqt, dq_b, dacc, near, dsend, r_m, r_b, y_b, y_c, ry1, ry2, own_b,
           kv_s, kv_r, q_s, q_r, g_s, g_r, loc,
           xm_s, xm_r, xb_s, xb_r, y_s, y_r,
           dm_s, dm_r, db_s, db_r, dy_s, dy_r,
           oa_s, oa_r, oq_s, oq_r, ok_s, ok_r):
    stretch = kvs.shape[2]
    scale = HEAD_DIM ** -0.5
    gw = group * HEAD_DIM
    c = lax.axis_index("ctx")
    p = lax.axis_index("tp")
    row = c // NX
    x = lax.rem(c, NX)

    def tp_at(i):
        return lax.rem(p + i, tp_n)

    def flip(r, t):
        return t + lax.rem(r // (rows_n // 2), 2) * (tp_n - 2 - 4 * (t // 2))

    def head_at(t):
        return flip(row, t)

    me = head_at(p)

    def mate_x(i):
        return lax.rem(x + i, NX)

    def ctx_at(r, xx):
        return r * NX + xx

    def row_at(k):
        return {"ctx": c + k * NX, "tp": flip(row + k, me)}

    def rcopy(src, dst, ss, rs, dev):
        return pltpu.make_async_remote_copy(
            src_ref=src, dst_ref=dst, send_sem=ss, recv_sem=rs, device_id=dev, device_id_type=MESH)

    barrier = pltpu.get_barrier_semaphore()
    for i in range(1, tp_n):
        pl.semaphore_signal(barrier, inc=1, device_id={"ctx": c, "tp": tp_at(i)}, device_id_type=MESH)
    for i in range(1, NX):
        pl.semaphore_signal(barrier, inc=1, device_id={"ctx": ctx_at(row, mate_x(i)), "tp": p}, device_id_type=MESH)
    for k in (1, 2, rows_n - 1, rows_n - 2):
        r = lax.rem(row + k, rows_n)
        pl.semaphore_signal(
            barrier, inc=1, device_id={"ctx": ctx_at(r, x), "tp": flip(r, me)}, device_id_type=MESH)
    pl.semaphore_wait(barrier, tp_n - 1 + NX - 1 + 4)

    my_rows = pl.ds(pl.multiple_of(p * tok, tok), tok)

    def cols(t, w):
        return pl.ds(pl.multiple_of(t * w, w), w)

    kv_copies = []
    for i in range(1, tp_n):
        t = tp_at(i)
        for n, src in ((0, k_in), (1, v_in)):
            cp = rcopy(src.at[:, cols(head_at(t), HEAD_DIM)], kvs.at[x, n, my_rows, :], kv_s.at[n, i - 1], kv_r.at[n, i - 1],
                       {"ctx": c, "tp": t})
            cp.start()
            kv_copies.append(cp)
    locals_ = [
        pltpu.make_async_copy(k_in.at[:, cols(me, HEAD_DIM)], kvs.at[x, 0, my_rows, :], loc.at[0]),
        pltpu.make_async_copy(v_in.at[:, cols(me, HEAD_DIM)], kvs.at[x, 1, my_rows, :], loc.at[1]),
        pltpu.make_async_copy(q_in.at[:, cols(me, gw)], qh.at[my_rows, :], loc.at[2]),
        pltpu.make_async_copy(g_in.at[:, cols(me, gw)], gh.at[my_rows, :], loc.at[3]),
    ]
    for cp in locals_:
        cp.start()
    q_copies = []
    for i in range(1, tp_n):
        t = tp_at(i)
        cp = rcopy(q_in.at[:, cols(head_at(t), gw)], qh.at[my_rows, :], q_s.at[i - 1], q_r.at[i - 1], {"ctx": c, "tp": t})
        q_copies.append(cp)
    mid = rows_n // 2
    out_z = (row == mid - 1) | (row == mid - 2)
    back_z = (row == mid) | (row == mid + 1)

    @pl.when(jnp.logical_not(out_z))
    def _():
        for cp in q_copies:
            cp.start()

    @pl.when(row < 2)
    def _():
        for i in range(1, NX):
            @pl.when(mate_x(i) > x)
            def _():
                kvs[mate_x(i)] = jnp.zeros(kvs.shape[1:], BF16)

    @pl.when(row < 1)
    def _():
        kvs[NX:] = jnp.zeros((NX,) + kvs.shape[1:], BF16)

    lane = lax.broadcasted_iota(jnp.int32, (1, stretch), 1)
    per = stretch // BLOCK
    q_doc = [docs[c * per + b] for b in range(per)]
    for slot in range(2 * NX):
        xs = slot % NX
        if slot < NX:
            src = jnp.where(xs <= x, c - x + xs, c - x + xs - 2 * NX)
        else:
            src = c - x + xs - NX
        own = (src == c).astype(jnp.int32)
        for b in range(per):
            k_doc = jnp.where(src >= 0, docs[jnp.maximum(src, 0) * per + b], -1)
            line = jnp.where(lane < BLOCK, jnp.where(k_doc == q_doc[0], 0.0, NEG), jnp.where(k_doc == q_doc[1], 0.0, NEG))
            key_at = lax.broadcasted_iota(jnp.int32, (BLOCK, stretch), 0) + b * BLOCK
            q_at = lax.broadcasted_iota(jnp.int32, (BLOCK, stretch), 1)
            late = (key_at - q_at) * own > 0
            bias[slot, b * BLOCK:(b + 1) * BLOCK, :] = jnp.where(late, NEG, jnp.broadcast_to(line, (BLOCK, stretch)))

    locals_[0].wait()
    locals_[1].wait()
    for cp in kv_copies:
        cp.wait_recv()

    def x_own(i):
        return rcopy(kvs.at[x], kvs.at[x], xm_s.at[i - 1], xm_r.at[i - 1], {"ctx": ctx_at(row, mate_x(i)), "tp": p})

    def x_far(i):
        return rcopy(cbuf, kvs.at[x], xm_s.at[i - 1], xm_r.at[i - 1], {"ctx": ctx_at(row, mate_x(i)), "tp": p})

    def x_prev(i):
        return rcopy(kvs.at[NX + x], kvs.at[NX + x], xb_s.at[i - 1], xb_r.at[i - 1],
                     {"ctx": ctx_at(row, mate_x(i)), "tp": p})

    to_next = rcopy(kvs.at[x], kvs.at[NX + x], y_s.at[0], y_r.at[0], row_at(1))
    to_second = rcopy(kvs.at[x], cbuf, y_s.at[1], y_r.at[1], row_at(2))
    has_next = row + 1 < rows_n
    has_second = (row + 2 < rows_n) & (x > 0)
    from_prev = row >= 1
    from_second = (row >= 2) & (x > 0)

    @pl.when(has_next)
    def _():
        to_next.start()

    @pl.when(has_second)
    def _():
        to_second.start()

    for i in range(1, NX):
        @pl.when(mate_x(i) > x)
        def _():
            x_own(i).start()

    @pl.when(out_z)
    def _():
        for cp in q_copies:
            cp.start()

    g_copies = []
    for i in range(1, tp_n):
        t = tp_at(i)
        cp = rcopy(g_in.at[:, cols(head_at(t), gw)], gh.at[my_rows, :], g_s.at[i - 1], g_r.at[i - 1], {"ctx": c, "tp": t})
        cp.start()
        g_copies.append(cp)

    @pl.when(from_prev)
    def _():
        to_next.wait_recv()
        for i in range(1, NX):
            x_prev(i).start()

    @pl.when(from_second)
    def _():
        to_second.wait_recv()
        for i in range(1, NX):
            @pl.when(mate_x(i) < x)
            def _():
                x_far(i).start()

    for i in range(1, NX):
        @pl.when((lax.rem(x + NX - i, NX) < x) | (row >= 2))
        def _():
            x_own(i).wait_recv()

    @pl.when(from_prev)
    def _():
        for i in range(1, NX):
            x_prev(i).wait_recv()

    for slot in range(2 * NX):
        kt[:, slot * stretch:(slot + 1) * stretch] = jnp.transpose(kvs[slot, 0].astype(F32)).astype(BF16)
        vt[:, slot * stretch:(slot + 1) * stretch] = jnp.transpose(kvs[slot, 1].astype(F32)).astype(BF16)

    locals_[2].wait()
    for cp in q_copies:
        cp.wait_recv()

    def forward(h, carry):
        at = pl.ds(pl.multiple_of(h * HEAD_DIM, HEAD_DIM), HEAD_DIM)
        q = qh[:, at]
        total = jnp.zeros((1, stretch), F32)
        out_t = jnp.zeros((HEAD_DIM, stretch), F32)
        for slot in range(2 * NX):
            s = dot(kvs[slot, 0], q, NT)
            w = jnp.exp2(s * (scale * LOG2E) + bias[slot])
            wts[h, slot] = w
            total = total + jnp.sum(w, axis=0, keepdims=True)
            out_t = out_t + dot(vt[:, slot * stretch:(slot + 1) * stretch], w.astype(BF16))
        inv_t[h] = 1.0 / total
        attn_b[:, at] = jnp.transpose(out_t / total).astype(BF16)
        return carry

    lax.fori_loop(0, group, forward, 0)

    a_copies = []
    for i in range(1, tp_n):
        t = tp_at(i)
        cp = rcopy(attn_b.at[cols(t, tok), :], attn_out.at[:, cols(me, gw)], oa_s.at[i - 1], oa_r.at[i - 1],
                   {"ctx": c, "tp": t})
        cp.start()
        a_copies.append(cp)
    keep_a = pltpu.make_async_copy(attn_b.at[my_rows, :], attn_out.at[:, cols(me, gw)], loc.at[0])
    keep_a.start()

    locals_[3].wait()
    for cp in g_copies:
        cp.wait_recv()

    def dots(h, carry):
        at = pl.ds(pl.multiple_of(h * HEAD_DIM, HEAD_DIM), HEAD_DIM)
        prod = gh[:, at].astype(F32) * attn_b[:, at].astype(F32)
        odot[h] = jnp.sum(jnp.transpose(prod), axis=0, keepdims=True)
        return carry

    lax.fori_loop(0, group, dots, 0)

    def d_m(i):
        return rcopy(dsend.at[mate_x(i)], r_m.at[i - 1], dm_s.at[i - 1], dm_r.at[i - 1],
                     {"ctx": ctx_at(row, mate_x(i)), "tp": p})

    def d_b(i):
        return rcopy(dsend.at[NX + mate_x(i)], r_b.at[i - 1], db_s.at[i - 1], db_r.at[i - 1],
                     {"ctx": ctx_at(row, mate_x(i)), "tp": p})

    half = group // 2
    hw = half * HEAD_DIM

    def grads(h, slot, q, g, k_t):
        pr = wts[h, slot] * inv_t[h]
        dp = dot(kvs[slot, 1], g, NT)
        ds = (pr * (dp - odot[h])).astype(BF16)
        return dot(ds, q), dot(pr.astype(BF16), g), dot(k_t, ds)

    def put_dq(h, total):
        at = pl.ds(pl.multiple_of(h * HEAD_DIM, HEAD_DIM), HEAD_DIM)
        dq_b[:, at] = (jnp.transpose(total) * scale).astype(BF16)

    dacc[...] = jnp.zeros_like(dacc)

    def first(h, carry):
        at = pl.ds(pl.multiple_of(h * HEAD_DIM, HEAD_DIM), HEAD_DIM)
        q = qh[:, at]
        g = gh[:, at]
        total = jnp.zeros((HEAD_DIM, stretch), F32)
        for slot in range(2 * NX):
            dk, dv, dq = grads(h, slot, q, g, kt[:, slot * stretch:(slot + 1) * stretch])
            dacc[slot, 0] += dk
            dacc[slot, 1] += dv
            total = total + dq
        put_dq(h, total)
        dqt[h] = jnp.zeros((HEAD_DIM, stretch), F32)
        return carry

    lax.fori_loop(0, half, first, 0)

    dq_copies = []
    for n in range(2):
        for i in range(1, tp_n):
            t = tp_at(i)
            to = pl.ds(pl.multiple_of(me * gw + n * hw, HEAD_DIM), hw)
            dq_copies.append(rcopy(
                dq_b.at[cols(t, tok), n * hw:(n + 1) * hw], dq_out.at[:, to], oq_s.at[n, i - 1], oq_r.at[n, i - 1],
                {"ctx": c, "tp": t}))
    for cp in dq_copies[:tp_n - 1]:
        cp.start()

    def backward(slot):
        k_t = kt[:, pl.ds(pl.multiple_of(slot * stretch, stretch), stretch)]

        def head(j, carry):
            h = half + j
            at = pl.ds(pl.multiple_of(h * HEAD_DIM, HEAD_DIM), HEAD_DIM)
            dk, dv, dq = grads(h, slot, qh[:, at], gh[:, at], k_t)
            dacc[slot, 0] += dk
            dacc[slot, 1] += dv
            dqt[j] += dq
            return carry

        lax.fori_loop(0, half, head, 0, unroll=True)

    def ready(slot):
        backward(slot)
        dsend[slot, 0] = (dacc[slot, 0] * scale).astype(BF16)
        dsend[slot, 1] = dacc[slot, 1].astype(BF16)

    for i in range(1, NX):
        ready(mate_x(i))
        d_m(i).start()
    for i in range(1, NX):
        ready(NX + mate_x(i))
        d_b(i).start()

    back_one = rcopy(y_b, ry1, dy_s.at[0], dy_r.at[0], row_at(-1))
    back_two = rcopy(y_c, ry2, dy_s.at[1], dy_r.at[1], row_at(-2))
    backward(x)
    for i in range(1, NX):
        d_m(i).wait_recv()
    far = jnp.zeros(near.shape, F32)
    near[0] = dacc[x, 0] * scale
    near[1] = dacc[x, 1]
    for i in range(1, NX):
        xs = lax.rem(x + NX - i, NX)
        got = r_m[i - 1].astype(F32)
        far = far + jnp.where(xs < x, got, 0.0)
        near[...] += jnp.where(xs > x, got, 0.0)
    y_c[...] = far.astype(BF16)

    @pl.when(from_second)
    def _():
        back_two.start()

    ready(NX + x)

    for j in range(half):
        put_dq(half + j, dqt[j])

    @pl.when(jnp.logical_not(back_z))
    def _():
        for cp in dq_copies[tp_n - 1:]:
            cp.start()

    for i in range(1, NX):
        d_b(i).wait_recv()
    y_b[...] = (dsend[NX + x].astype(F32) + r_b[0].astype(F32) + r_b[1].astype(F32) + r_b[2].astype(F32)).astype(BF16)

    @pl.when(from_prev)
    def _():
        back_one.start()

    @pl.when(back_z)
    def _():
        for cp in dq_copies[tp_n - 1:]:
            cp.start()

    keep_q = pltpu.make_async_copy(dq_b.at[my_rows, :], dq_out.at[:, cols(me, gw)], loc.at[1])
    keep_q.start()

    @pl.when(has_second)
    def _():
        back_two.wait_recv()
        near[...] += ry2[...].astype(F32)

    @pl.when(has_next)
    def _():
        back_one.wait_recv()
        near[...] += ry1[...].astype(F32)

    own_b[...] = near[...].astype(BF16)
    k_copies = []
    for i in range(1, tp_n):
        t = tp_at(i)
        cp = rcopy(own_b.at[:, cols(t, tok), :], dkv_out.at[:, :, cols(me, HEAD_DIM)], ok_s.at[i - 1], ok_r.at[i - 1],
                   {"ctx": c, "tp": t})
        cp.start()
        k_copies.append(cp)
    keep_k = pltpu.make_async_copy(own_b.at[:, my_rows, :], dkv_out.at[:, :, cols(me, HEAD_DIM)], loc.at[2])
    keep_k.start()

    for cp in a_copies + dq_copies + k_copies:
        cp.wait_recv()
    for cp in (keep_a, keep_q, keep_k):
        cp.wait()

    for cp in kv_copies + q_copies + g_copies + a_copies + dq_copies + k_copies:
        cp.wait_send()
    for i in range(1, NX):
        @pl.when((mate_x(i) > x) | (row >= 2))
        def _():
            x_own(i).wait_send()
        d_m(i).wait_send()
        d_b(i).wait_send()

    @pl.when(from_prev)
    def _():
        for i in range(1, NX):
            x_prev(i).wait_send()
        back_one.wait_send()

    @pl.when(from_second)
    def _():
        back_two.wait_send()

    @pl.when(has_next)
    def _():
        to_next.wait_send()

    @pl.when(has_second)
    def _():
        to_second.wait_send()


def solution(mesh):
    ctx_n, tp_n = mesh.shape["ctx"], mesh.shape["tp"]
    rows_n = ctx_n // NX

    def local(query_rows, key_rows, value_rows, doc_ids, grad_out):
        tok, width = query_rows.shape
        kw = key_rows.shape[1]
        stretch = tok * tp_n
        gw = width // tp_n
        group = gw // HEAD_DIM
        n2 = 2 * NX
        dma = pltpu.SemaphoreType.DMA
        piece = (2, stretch, HEAD_DIM)
        V = pltpu.VMEM
        anyspec = pl.BlockSpec(memory_space=pl.ANY)
        scratch = [
            V((stretch, gw), BF16), V((stretch, gw), BF16), V((n2,) + piece, BF16), V(piece, BF16),
            V((HEAD_DIM, n2 * stretch), BF16), V((HEAD_DIM, n2 * stretch), BF16), V((n2, stretch, stretch), F32),
            V((group, n2, stretch, stretch), F32), V((group, 1, stretch), F32), V((group, 1, stretch), F32),
            V((stretch, gw), BF16), V((group // 2, HEAD_DIM, stretch), F32), V((stretch, gw), BF16),
            V((n2,) + piece, F32), V(piece, F32), V((n2,) + piece, BF16), V((NX - 1,) + piece, BF16), V((NX - 1,) + piece, BF16),
            V(piece, BF16), V(piece, BF16), V(piece, BF16), V(piece, BF16), V(piece, BF16),
            dma((2, tp_n - 1)), dma((2, tp_n - 1)), dma((tp_n - 1,)), dma((tp_n - 1,)), dma((tp_n - 1,)),
            dma((tp_n - 1,)), dma((4,)),
            dma((NX - 1,)), dma((NX - 1,)), dma((NX - 1,)), dma((NX - 1,)), dma((2,)), dma((2,)),
            dma((NX - 1,)), dma((NX - 1,)), dma((NX - 1,)), dma((NX - 1,)), dma((2,)), dma((2,)),
            dma((tp_n - 1,)), dma((tp_n - 1,)), dma((2, tp_n - 1)), dma((2, tp_n - 1)), dma((tp_n - 1,)), dma((tp_n - 1,)),
        ]
        attn, dq, dkv = pl.pallas_call(
            functools.partial(kernel, rows_n, tp_n, group, tok),
            out_shape=(
                jax.ShapeDtypeStruct((tok, width), BF16),
                jax.ShapeDtypeStruct((tok, width), BF16),
                jax.ShapeDtypeStruct((2, tok, kw), BF16),
            ),
            in_specs=[pl.BlockSpec(memory_space=pltpu.SMEM)] + [anyspec] * 4,
            out_specs=(anyspec,) * 3,
            scratch_shapes=scratch,
            compiler_params=pltpu.CompilerParams(
                collective_id=0, has_side_effects=True, vmem_limit_bytes=60 * 1024 * 1024),
            name="attention_layer",
        )(doc_ids, query_rows, key_rows, value_rows, grad_out)
        return attn, dq.astype(F32), dkv[0].astype(F32), dkv[1].astype(F32)

    rows = P(("ctx", "tp"), None)
    return jax.shard_map(
        local, mesh=mesh, in_specs=(rows, rows, rows, P(), rows), out_specs=(rows,) * 4, check_vma=False)
```

```python
import functools
import jax
import jax.numpy as jnp
from jax import lax
from jax.experimental import pallas as pl
from jax.experimental.pallas import tpu as pltpu
from jax.sharding import PartitionSpec as P

HEAD_DIM = 128
BLOCK = 128
NX = 4
MESH = pl.DeviceIdType.MESH
LOG2E = 1.4426950408889634
NEG = -1e30
F32 = jnp.float32
BF16 = jnp.bfloat16
NT = (((1,), (1,)), ((), ()))
NN = (((1,), (0,)), ((), ()))


def dot(a, b, dims=NN):
    return lax.dot_general(a, b, dims, preferred_element_type=F32)


def kernel(rows_n, tp_n, group, tok, docs, q_in, k_in, v_in, g_in,
           attn_out, dq_out, dkv_out,
           qh, gh, kvs, cbuf, kt, vt, bias, wts, inv_t, odot,
           attn_b, dqt, dq_b, dacc, near, dsend, r_m, r_b, y_b, y_c, ry1, ry2, own_b,
           kv_s, kv_r, q_s, q_r, g_s, g_r, loc,
           xm_s, xm_r, xb_s, xb_r, y_s, y_r,
           dm_s, dm_r, db_s, db_r, dy_s, dy_r,
           oa_s, oa_r, oq_s, oq_r, ok_s, ok_r):
    stretch = kvs.shape[2]
    scale = HEAD_DIM ** -0.5
    gw = group * HEAD_DIM
    c = lax.axis_index("ctx")
    p = lax.axis_index("tp")
    row = c // NX
    x = lax.rem(c, NX)

    def tp_at(i):
        return lax.rem(p + i, tp_n)

    def flip(r, t):
        return t + lax.rem(r // (rows_n // 2), 2) * (tp_n - 2 - 4 * (t // 2))

    def head_at(t):
        return flip(row, t)

    me = head_at(p)

    def mate_x(i):
        return lax.rem(x + i, NX)

    def ctx_at(r, xx):
        return r * NX + xx

    def row_at(k):
        return {"ctx": c + k * NX, "tp": flip(row + k, me)}

    def rcopy(src, dst, ss, rs, dev):
        return pltpu.make_async_remote_copy(
            src_ref=src, dst_ref=dst, send_sem=ss, recv_sem=rs, device_id=dev, device_id_type=MESH)

    barrier = pltpu.get_barrier_semaphore()
    for i in range(1, tp_n):
        pl.semaphore_signal(barrier, inc=1, device_id={"ctx": c, "tp": tp_at(i)}, device_id_type=MESH)
    for i in range(1, NX):
        pl.semaphore_signal(barrier, inc=1, device_id={"ctx": ctx_at(row, mate_x(i)), "tp": p}, device_id_type=MESH)
    for k in (1, 2, rows_n - 1, rows_n - 2):
        r = lax.rem(row + k, rows_n)
        pl.semaphore_signal(
            barrier, inc=1, device_id={"ctx": ctx_at(r, x), "tp": flip(r, me)}, device_id_type=MESH)
    pl.semaphore_wait(barrier, tp_n - 1 + NX - 1 + 4)

    my_rows = pl.ds(pl.multiple_of(p * tok, tok), tok)

    def cols(t, w):
        return pl.ds(pl.multiple_of(t * w, w), w)

    kv_copies = []
    for i in range(1, tp_n):
        t = tp_at(i)
        for n, src in ((0, k_in), (1, v_in)):
            cp = rcopy(src.at[:, cols(head_at(t), HEAD_DIM)], kvs.at[x, n, my_rows, :], kv_s.at[n, i - 1], kv_r.at[n, i - 1],
                       {"ctx": c, "tp": t})
            cp.start()
            kv_copies.append(cp)
    locals_ = [
        pltpu.make_async_copy(k_in.at[:, cols(me, HEAD_DIM)], kvs.at[x, 0, my_rows, :], loc.at[0]),
        pltpu.make_async_copy(v_in.at[:, cols(me, HEAD_DIM)], kvs.at[x, 1, my_rows, :], loc.at[1]),
        pltpu.make_async_copy(q_in.at[:, cols(me, gw)], qh.at[my_rows, :], loc.at[2]),
        pltpu.make_async_copy(g_in.at[:, cols(me, gw)], gh.at[my_rows, :], loc.at[3]),
    ]
    for cp in locals_:
        cp.start()
    q_copies = []
    for i in range(1, tp_n):
        t = tp_at(i)
        cp = rcopy(q_in.at[:, cols(head_at(t), gw)], qh.at[my_rows, :], q_s.at[i - 1], q_r.at[i - 1], {"ctx": c, "tp": t})
        q_copies.append(cp)
    mid = rows_n // 2
    out_z = (row == mid - 1) | (row == mid - 2)
    back_z = (row == mid) | (row == mid + 1)

    @pl.when(jnp.logical_not(out_z))
    def _():
        for cp in q_copies:
            cp.start()

    @pl.when(row < 2)
    def _():
        for i in range(1, NX):
            @pl.when(mate_x(i) > x)
            def _():
                kvs[mate_x(i)] = jnp.zeros(kvs.shape[1:], BF16)

    @pl.when(row < 1)
    def _():
        kvs[NX:] = jnp.zeros((NX,) + kvs.shape[1:], BF16)

    lane = lax.broadcasted_iota(jnp.int32, (1, stretch), 1)
    per = stretch // BLOCK
    q_doc = [docs[c * per + b] for b in range(per)]
    for slot in range(2 * NX):
        xs = slot % NX
        if slot < NX:
            src = jnp.where(xs <= x, c - x + xs, c - x + xs - 2 * NX)
        else:
            src = c - x + xs - NX
        own = (src == c).astype(jnp.int32)
        for b in range(per):
            k_doc = jnp.where(src >= 0, docs[jnp.maximum(src, 0) * per + b], -1)
            line = jnp.where(lane < BLOCK, jnp.where(k_doc == q_doc[0], 0.0, NEG), jnp.where(k_doc == q_doc[1], 0.0, NEG))
            key_at = lax.broadcasted_iota(jnp.int32, (BLOCK, stretch), 0) + b * BLOCK
            q_at = lax.broadcasted_iota(jnp.int32, (BLOCK, stretch), 1)
            late = (key_at - q_at) * own > 0
            bias[slot, b * BLOCK:(b + 1) * BLOCK, :] = jnp.where(late, NEG, jnp.broadcast_to(line, (BLOCK, stretch)))

    locals_[0].wait()
    locals_[1].wait()
    for cp in kv_copies:
        cp.wait_recv()

    def x_own(i):
        return rcopy(kvs.at[x], kvs.at[x], xm_s.at[i - 1], xm_r.at[i - 1], {"ctx": ctx_at(row, mate_x(i)), "tp": p})

    def x_far(i):
        return rcopy(cbuf, kvs.at[x], xm_s.at[i - 1], xm_r.at[i - 1], {"ctx": ctx_at(row, mate_x(i)), "tp": p})

    def x_prev(i):
        return rcopy(kvs.at[NX + x], kvs.at[NX + x], xb_s.at[i - 1], xb_r.at[i - 1],
                     {"ctx": ctx_at(row, mate_x(i)), "tp": p})

    left, right = mate_x(NX - 1), mate_x(1)
    pass_k = rcopy(kvs.at[NX + left, 0], kvs.at[NX + left, 0], xb_s.at[1], xb_r.at[1],
                   {"ctx": ctx_at(row, right), "tp": p})
    pass_v = rcopy(kvs.at[NX + right, 1], kvs.at[NX + right, 1], xb_s.at[3], xb_r.at[3],
                   {"ctx": ctx_at(row, left), "tp": p})
    to_next = rcopy(kvs.at[x], kvs.at[NX + x], y_s.at[0], y_r.at[0], row_at(1))
    to_second = rcopy(kvs.at[x], cbuf, y_s.at[1], y_r.at[1], row_at(2))
    has_next = row + 1 < rows_n
    has_second = (row + 2 < rows_n) & (x > 0)
    from_prev = row >= 1
    from_second = (row >= 2) & (x > 0)

    @pl.when(has_next)
    def _():
        to_next.start()

    @pl.when(has_second)
    def _():
        to_second.start()

    for i in range(1, NX):
        @pl.when(mate_x(i) > x)
        def _():
            x_own(i).start()

    @pl.when(out_z)
    def _():
        for cp in q_copies:
            cp.start()

    half = group // 2
    hw = half * HEAD_DIM

    def part(t, n):
        return pl.ds(pl.multiple_of(t * gw + n * hw, HEAD_DIM), hw)

    g_copies = []
    for n in range(2):
        for i in range(1, tp_n):
            t = tp_at(i)
            cp = rcopy(g_in.at[:, part(head_at(t), n)], gh.at[my_rows, n * hw:(n + 1) * hw], g_s.at[n, i - 1],
                       g_r.at[n, i - 1], {"ctx": c, "tp": t})
            cp.start()
            g_copies.append(cp)

    @pl.when(from_prev)
    def _():
        to_next.wait_recv()
        x_prev(1).start()
        x_prev(NX - 1).start()

    @pl.when(from_second)
    def _():
        to_second.wait_recv()
        for i in range(1, NX):
            @pl.when(mate_x(i) < x)
            def _():
                x_far(i).start()

    @pl.when(from_prev)
    def _():
        x_prev(1).wait_recv()
        pass_k.start()
        x_prev(NX - 1).wait_recv()
        pass_v.start()

    for i in range(1, NX):
        @pl.when((lax.rem(x + NX - i, NX) < x) | (row >= 2))
        def _():
            x_own(i).wait_recv()

    @pl.when(from_prev)
    def _():
        pass_k.wait_recv()
        pass_v.wait_recv()

    for slot in range(2 * NX):
        kt[:, slot * stretch:(slot + 1) * stretch] = jnp.transpose(kvs[slot, 0].astype(F32)).astype(BF16)
        vt[:, slot * stretch:(slot + 1) * stretch] = jnp.transpose(kvs[slot, 1].astype(F32)).astype(BF16)

    locals_[2].wait()
    for cp in q_copies:
        cp.wait_recv()

    def forward(h, carry):
        at = pl.ds(pl.multiple_of(h * HEAD_DIM, HEAD_DIM), HEAD_DIM)
        q = qh[:, at]
        total = jnp.zeros((1, stretch), F32)
        out_t = jnp.zeros((HEAD_DIM, stretch), F32)
        for slot in range(2 * NX):
            s = dot(kvs[slot, 0], q, NT)
            w = jnp.exp2(s * (scale * LOG2E) + bias[slot])
            wts[h, slot] = w
            total = total + jnp.sum(w, axis=0, keepdims=True)
            out_t = out_t + dot(vt[:, slot * stretch:(slot + 1) * stretch], w.astype(BF16))
        inv_t[h] = 1.0 / total
        attn_b[:, at] = jnp.transpose(out_t / total).astype(BF16)
        return carry

    a_copies = []
    for n in range(2):
        lax.fori_loop(n * half, (n + 1) * half, forward, 0)
        for i in range(1, tp_n):
            t = tp_at(i)
            cp = rcopy(attn_b.at[cols(t, tok), n * hw:(n + 1) * hw], attn_out.at[:, part(me, n)], oa_s.at[n, i - 1],
                       oa_r.at[n, i - 1], {"ctx": c, "tp": t})
            cp.start()
            a_copies.append(cp)
    keep_a = pltpu.make_async_copy(attn_b.at[my_rows, :], attn_out.at[:, cols(me, gw)], loc.at[0])
    keep_a.start()

    locals_[3].wait()
    for cp in g_copies[:tp_n - 1]:
        cp.wait_recv()

    def dots(h, carry):
        at = pl.ds(pl.multiple_of(h * HEAD_DIM, HEAD_DIM), HEAD_DIM)
        prod = gh[:, at].astype(F32) * attn_b[:, at].astype(F32)
        odot[h] = jnp.sum(jnp.transpose(prod), axis=0, keepdims=True)
        return carry

    lax.fori_loop(0, half, dots, 0)

    def d_m(i):
        return rcopy(dsend.at[mate_x(i)], r_m.at[i - 1], dm_s.at[i - 1], dm_r.at[i - 1],
                     {"ctx": ctx_at(row, mate_x(i)), "tp": p})

    def d_b(i):
        return rcopy(dsend.at[NX + mate_x(i)], r_b.at[i - 1], db_s.at[i - 1], db_r.at[i - 1],
                     {"ctx": ctx_at(row, mate_x(i)), "tp": p})

    def grads(h, slot, q, g, k_t):
        pr = wts[h, slot] * inv_t[h]
        dp = dot(kvs[slot, 1], g, NT)
        ds = (pr * (dp - odot[h])).astype(BF16)
        return dot(ds, q), dot(pr.astype(BF16), g), dot(k_t, ds)

    def put_dq(h, total):
        at = pl.ds(pl.multiple_of(h * HEAD_DIM, HEAD_DIM), HEAD_DIM)
        dq_b[:, at] = (jnp.transpose(total) * scale).astype(BF16)

    dacc[...] = jnp.zeros_like(dacc)

    def first(h, carry):
        at = pl.ds(pl.multiple_of(h * HEAD_DIM, HEAD_DIM), HEAD_DIM)
        q = qh[:, at]
        g = gh[:, at]
        total = jnp.zeros((HEAD_DIM, stretch), F32)
        for slot in range(2 * NX):
            dk, dv, dq = grads(h, slot, q, g, kt[:, slot * stretch:(slot + 1) * stretch])
            dacc[slot, 0] += dk
            dacc[slot, 1] += dv
            total = total + dq
        put_dq(h, total)
        dqt[h] = jnp.zeros((HEAD_DIM, stretch), F32)
        return carry

    lax.fori_loop(0, half, first, 0)

    dq_copies = []
    for n in range(2):
        for i in range(1, tp_n):
            t = tp_at(i)
            dq_copies.append(rcopy(
                dq_b.at[cols(t, tok), n * hw:(n + 1) * hw], dq_out.at[:, part(me, n)], oq_s.at[n, i - 1], oq_r.at[n, i - 1],
                {"ctx": c, "tp": t}))
    for cp in dq_copies[:tp_n - 1]:
        cp.start()

    for cp in g_copies[tp_n - 1:]:
        cp.wait_recv()
    lax.fori_loop(half, group, dots, 0)

    def backward(slot):
        k_t = kt[:, pl.ds(pl.multiple_of(slot * stretch, stretch), stretch)]

        def head(j, carry):
            h = half + j
            at = pl.ds(pl.multiple_of(h * HEAD_DIM, HEAD_DIM), HEAD_DIM)
            dk, dv, dq = grads(h, slot, qh[:, at], gh[:, at], k_t)
            dacc[slot, 0] += dk
            dacc[slot, 1] += dv
            dqt[j] += dq
            return carry

        lax.fori_loop(0, half, head, 0, unroll=True)

    def ready(slot):
        backward(slot)
        dsend[slot, 0] = (dacc[slot, 0] * scale).astype(BF16)
        dsend[slot, 1] = dacc[slot, 1].astype(BF16)

    for i in range(1, NX):
        ready(mate_x(i))
        d_m(i).start()
    for i in range(1, NX):
        ready(NX + mate_x(i))
        d_b(i).start()

    back_one = rcopy(y_b, ry1, dy_s.at[0], dy_r.at[0], row_at(-1))
    back_two = rcopy(y_c, ry2, dy_s.at[1], dy_r.at[1], row_at(-2))
    backward(x)
    for i in range(1, NX):
        d_m(i).wait_recv()
    far = jnp.zeros(near.shape, F32)
    near[0] = dacc[x, 0] * scale
    near[1] = dacc[x, 1]
    for i in range(1, NX):
        xs = lax.rem(x + NX - i, NX)
        got = r_m[i - 1].astype(F32)
        far = far + jnp.where(xs < x, got, 0.0)
        near[...] += jnp.where(xs > x, got, 0.0)
    y_c[...] = far.astype(BF16)

    @pl.when(from_second)
    def _():
        back_two.start()

    ready(NX + x)

    for j in range(half):
        put_dq(half + j, dqt[j])

    @pl.when(jnp.logical_not(back_z))
    def _():
        for cp in dq_copies[tp_n - 1:]:
            cp.start()

    for i in range(1, NX):
        d_b(i).wait_recv()
    y_b[...] = (dsend[NX + x].astype(F32) + r_b[0].astype(F32) + r_b[1].astype(F32) + r_b[2].astype(F32)).astype(BF16)

    @pl.when(from_prev)
    def _():
        back_one.start()

    @pl.when(back_z)
    def _():
        for cp in dq_copies[tp_n - 1:]:
            cp.start()

    keep_q = pltpu.make_async_copy(dq_b.at[my_rows, :], dq_out.at[:, cols(me, gw)], loc.at[1])
    keep_q.start()

    @pl.when(has_second)
    def _():
        back_two.wait_recv()
        near[...] += ry2[...].astype(F32)

    @pl.when(has_next)
    def _():
        back_one.wait_recv()
        near[...] += ry1[...].astype(F32)

    own_b[...] = near[...].astype(BF16)
    k_copies = []
    for i in range(1, tp_n):
        t = tp_at(i)
        cp = rcopy(own_b.at[:, cols(t, tok), :], dkv_out.at[:, :, cols(me, HEAD_DIM)], ok_s.at[i - 1], ok_r.at[i - 1],
                   {"ctx": c, "tp": t})
        cp.start()
        k_copies.append(cp)
    keep_k = pltpu.make_async_copy(own_b.at[:, my_rows, :], dkv_out.at[:, :, cols(me, HEAD_DIM)], loc.at[2])
    keep_k.start()

    for cp in a_copies + dq_copies + k_copies:
        cp.wait_recv()
    for cp in (keep_a, keep_q, keep_k):
        cp.wait()

    for cp in kv_copies + q_copies + g_copies + a_copies + dq_copies + k_copies:
        cp.wait_send()
    for i in range(1, NX):
        @pl.when((mate_x(i) > x) | (row >= 2))
        def _():
            x_own(i).wait_send()
        d_m(i).wait_send()
        d_b(i).wait_send()

    @pl.when(from_prev)
    def _():
        x_prev(1).wait_send()
        x_prev(NX - 1).wait_send()
        pass_k.wait_send()
        pass_v.wait_send()
        back_one.wait_send()

    @pl.when(from_second)
    def _():
        back_two.wait_send()

    @pl.when(has_next)
    def _():
        to_next.wait_send()

    @pl.when(has_second)
    def _():
        to_second.wait_send()


def solution(mesh):
    ctx_n, tp_n = mesh.shape["ctx"], mesh.shape["tp"]
    rows_n = ctx_n // NX

    def local(query_rows, key_rows, value_rows, doc_ids, grad_out):
        tok, width = query_rows.shape
        kw = key_rows.shape[1]
        stretch = tok * tp_n
        gw = width // tp_n
        group = gw // HEAD_DIM
        n2 = 2 * NX
        dma = pltpu.SemaphoreType.DMA
        piece = (2, stretch, HEAD_DIM)
        V = pltpu.VMEM
        anyspec = pl.BlockSpec(memory_space=pl.ANY)
        scratch = [
            V((stretch, gw), BF16), V((stretch, gw), BF16), V((n2,) + piece, BF16), V(piece, BF16),
            V((HEAD_DIM, n2 * stretch), BF16), V((HEAD_DIM, n2 * stretch), BF16), V((n2, stretch, stretch), F32),
            V((group, n2, stretch, stretch), F32), V((group, 1, stretch), F32), V((group, 1, stretch), F32),
            V((stretch, gw), BF16), V((group // 2, HEAD_DIM, stretch), F32), V((stretch, gw), BF16),
            V((n2,) + piece, F32), V(piece, F32), V((n2,) + piece, BF16), V((NX - 1,) + piece, BF16), V((NX - 1,) + piece, BF16),
            V(piece, BF16), V(piece, BF16), V(piece, BF16), V(piece, BF16), V(piece, BF16),
            dma((2, tp_n - 1)), dma((2, tp_n - 1)), dma((tp_n - 1,)), dma((tp_n - 1,)), dma((2, tp_n - 1)),
            dma((2, tp_n - 1)), dma((4,)),
            dma((NX - 1,)), dma((NX - 1,)), dma((NX,)), dma((NX,)), dma((2,)), dma((2,)),
            dma((NX - 1,)), dma((NX - 1,)), dma((NX - 1,)), dma((NX - 1,)), dma((2,)), dma((2,)),
            dma((2, tp_n - 1)), dma((2, tp_n - 1)), dma((2, tp_n - 1)), dma((2, tp_n - 1)), dma((tp_n - 1,)), dma((tp_n - 1,)),
        ]
        attn, dq, dkv = pl.pallas_call(
            functools.partial(kernel, rows_n, tp_n, group, tok),
            out_shape=(
                jax.ShapeDtypeStruct((tok, width), BF16),
                jax.ShapeDtypeStruct((tok, width), BF16),
                jax.ShapeDtypeStruct((2, tok, kw), BF16),
            ),
            in_specs=[pl.BlockSpec(memory_space=pltpu.SMEM)] + [anyspec] * 4,
            out_specs=(anyspec,) * 3,
            scratch_shapes=scratch,
            compiler_params=pltpu.CompilerParams(
                collective_id=0, has_side_effects=True, vmem_limit_bytes=60 * 1024 * 1024),
            name="attention_layer",
        )(doc_ids, query_rows, key_rows, value_rows, grad_out)
        return attn, dq.astype(F32), dkv[0].astype(F32), dkv[1].astype(F32)

    rows = P(("ctx", "tp"), None)
    return jax.shard_map(
        local, mesh=mesh, in_specs=(rows, rows, rows, P(), rows), out_specs=(rows,) * 4, check_vma=False)
```
